256 devices in a mesh: req: 32 (over z, x), mlp: 8 (over y, core).
Axes of the slice: x: 4, y: 4, z: 8, core: 2. Of those that a mesh axis runs over, the one named last changes fastest.
Arguments:
- tokens: bfloat16 [8192, 2048], P('req', 'mlp'), may hold values from -12 to 12
- segment_ids: int32 [8192], P('req'), may hold values from 0 to 16, never falling along the last dimension, each value on 1 to 4096 neighbouring positions
- page_source: int32 [512], P('req'), may hold values from 0 to 511, each once
- query_weight: bfloat16 [2048, 2048], P(None, 'mlp')
- key_weight: bfloat16 [2048, 2048], P(None, 'mlp')
- value_weight: bfloat16 [2048, 2048], P(None, 'mlp'), may hold values from -0.125 to 0.125
- out_weight: bfloat16 [2048, 2048], P('mlp')
- query_gain: float32 [2048], P('mlp'), may hold values from 0.5 to 9
- key_gain: float32 [2048], P('mlp'), may hold values from 0.5 to 9
- attention_gain: float32 [2048], P('mlp'), may hold values from 0.25 to 1.75
- gate_weight: bfloat16 [2048, 8192], P('req', 'mlp'), may hold values from -0.125 to 0.125
- up_weight: bfloat16 [2048, 8192], P('req', 'mlp'), may hold values from -0.125 to 0.125
- down_weight: bfloat16 [2048, 8192], P('req', 'mlp')
- feedforward_gain: float32 [2048], P('mlp'), may hold values from 0.25 to 1.75
Outputs:
- layer_out: bfloat16 [8192, 2048], P('req', 'mlp')
- page_cache: bfloat16 [512, 2, 16, 2048], P('req', None, None, 'mlp')
The draws below stay inside these ranges and needn't reach their ends.
Inputs may be any that keep to these rules, and one draw needn't show every extreme that they name: `segment_ids`: segment ids never fall along the stream; each prompt has 1 to 4096 tokens and one has exactly 4096. `page_source`: each stream page appears once.
All inputs are finite; a program needn't handle non-finite values.
Results may differ from the reference program's by a relative error of at most 0.019.
The reference program's roundings to bfloat16 on the way (of `attended`, `residual` and `hidden`) count: a program that leaves them out, or rounds other values in their place, can miss the bound.
Values may be sent and summed in bfloat16 or wider, within the bound.
No kernel may reach another device: no remote copies, remote signals or barrier semaphores. Data moves between devices by JAX's collectives and lax.ppermute only.
A program may use at most 128 MiB of HBM per device.

```python
import math
import jax
import jax.numpy as jnp
import numpy as np
from jax import lax

D = 2048
H = 16
HD = 128
FF = 8192
PAGE = 16
TOK_DEV = 256
TOKENS = 8192
SEGS = 17
LONG = 4096
PAGES = 512


def trend_scale(rng_key, size_n):
    position_frac = jnp.arange(size_n, dtype=jnp.float32) / size_n
    random_part = jnp.exp(jax.random.uniform(rng_key, (size_n,), jnp.float32, 0.0, math.log(4.0)))
    return jnp.exp(position_frac * math.log(3.0)) * random_part


def projection(rng_key, fan_in, shape, out_dim):
    first_key, second_key = jax.random.split(rng_key)
    base_vals = jnp.clip(jax.random.normal(first_key, shape, jnp.float32), -4.0, 4.0)
    scales = trend_scale(second_key, shape[out_dim])
    if out_dim == 1:
        scaled = base_vals * scales[None, :]
    else:
        scaled = base_vals * scales[:, None]
    return (scaled / math.sqrt(fan_in)).astype(jnp.bfloat16)


def head_gain(rng_key, salt):
    feature_key = jax.random.fold_in(rng_key, salt)
    noise = jnp.clip(jax.random.normal(feature_key, (D,), jnp.float32), -3.0, 3.0)
    return 1.0 + 0.15 * noise


def draw_tokens(key, part):
    first_key, second_key = jax.random.split(jax.random.fold_in(key, 11))
    base_vals = jnp.clip(jax.random.normal(first_key, (TOKENS, D), jnp.float32), -4.0, 4.0)
    row_scale = jnp.exp(jax.random.uniform(second_key, (TOKENS, 1), jnp.float32, math.log(0.3), math.log(3.0)))
    return (base_vals * row_scale).astype(jnp.bfloat16)


def draw_query_weight(key, part):
    return projection(jax.random.fold_in(key, 21), D, (D, D), 1)


def draw_key_weight(key, part):
    return projection(jax.random.fold_in(key, 22), D, (D, D), 1)


def draw_out_weight(key, part):
    return projection(jax.random.fold_in(key, 23), D, (D, D), 1)


def draw_down_weight(key, part):
    return projection(jax.random.fold_in(key, 24), FF, (D, FF), 0)


def draw_query_gain(key, part):
    return head_gain(key, 31)


def draw_key_gain(key, part):
    return head_gain(key, 32)


def block_levels(stream_key, shape, pieces, smallest, high):
    level, own = 1.0, jax.random.fold_in(stream_key, 6)
    for dim, blocks in pieces:
        draws = jnp.exp(jax.random.uniform(jax.random.fold_in(own, dim), (blocks,), jnp.float32, smallest / len(pieces), high / len(pieces)))
        level = level * jnp.repeat(draws, shape[dim] // blocks).reshape([-1 if axis == dim else 1 for axis in range(len(shape))])
    return level


def split_up(amount, total, bound, skew):
    portions = [(1 << 20) // math.isqrt(grade ** skew) + 1 for grade in range(2, amount + 1)]
    rest, holding = total - bound - (amount - 1), [1] * (amount - 1)
    while rest > 0:
        candidates = [i for i in range(amount - 1) if holding[i] < bound]
        whole, left = sum([portions[i] for i in candidates]), rest
        for i in candidates:
            extra = min(bound - holding[i], max(1, left * portions[i] // whole), rest)
            holding[i] = holding[i] + extra
            rest = rest - extra
    return np.array([bound] + holding)


def ragged(rng, number_of, total, most, slope):
    if number_of == 2:
        one = jax.random.randint(rng, (), max(1, total - most), min(most, total - 1) + 1)
        return jnp.stack([one, total - one])
    lengths = jnp.asarray(split_up(number_of, total, most, slope), jnp.int32)
    twos = (number_of - 1) // 2
    giver, sink = lengths[1:1 + 2 * twos:2], lengths[2:2 + 2 * twos:2]
    slack = jnp.minimum(giver - 1, most - sink)
    passed = jax.random.randint(jax.random.fold_in(rng, 1), (twos,), 0, 1 << 20) % (slack + 1)
    lengths = lengths.at[1:1 + 2 * twos:2].set(giver - passed).at[2:2 + 2 * twos:2].set(sink + passed)
    return lengths[jax.random.permutation(jax.random.fold_in(rng, 2), number_of)]


def normal_values(stream_key, dims, scale, bound, shards=(), kind=jnp.bfloat16):
    gain = block_levels(stream_key, dims, shards, -0.22, 0.18) if shards else 1.0
    drawn = jax.random.normal(stream_key, dims, jnp.float32) * scale * gain
    return jnp.minimum(jnp.maximum(drawn, -bound), bound).astype(kind)


def setup_inputs(seed: int = 0) -> dict:
    streams_of = jax.random.split(jax.random.key(seed), 15)
    return {
        "tokens": draw_tokens(jax.random.fold_in(streams_of[14], 71), 0),
        "segment_ids": jnp.searchsorted(jnp.cumsum(ragged(streams_of[1], SEGS, TOKENS, LONG, 1)), jnp.arange(TOKENS), side="right").astype(jnp.int32),
        "page_source": jax.random.permutation(streams_of[2], PAGES).astype(jnp.int32),
        "query_weight": draw_query_weight(jax.random.fold_in(streams_of[14], 71), 0),
        "key_weight": draw_key_weight(jax.random.fold_in(streams_of[14], 71), 0),
        "value_weight": normal_values(streams_of[5], (D, D), D ** -0.5, 0.125, ((1, 8),)),
        "out_weight": draw_out_weight(jax.random.fold_in(streams_of[14], 71), 0),
        "query_gain": draw_query_gain(jax.random.fold_in(streams_of[14], 71), 0),
        "key_gain": draw_key_gain(jax.random.fold_in(streams_of[14], 71), 0),
        "attention_gain": jnp.clip(1.0 + 0.15 * jax.random.normal(streams_of[9], (D,), jnp.float32), 0.25, 1.75),
        "gate_weight": normal_values(streams_of[10], (D, FF), D ** -0.5, 0.125, ((0, 32), (1, 8))),
        "up_weight": normal_values(streams_of[11], (D, FF), D ** -0.5, 0.125, ((0, 32), (1, 8))),
        "down_weight": draw_down_weight(jax.random.fold_in(streams_of[14], 71), 0),
        "feedforward_gain": jnp.clip(1.0 + 0.15 * jax.random.normal(streams_of[13], (D,), jnp.float32), 0.25, 1.75),
    }


rope_base = 500000.0
norm_eps = 1e-06

def rope_tables(positions, head_dim):
    half_dim = head_dim // 2
    inv_freq = rope_base ** (-(jnp.arange(half_dim, dtype=jnp.float32) * 2.0) / head_dim)
    angles = positions.astype(jnp.float32)[:, None] * inv_freq[None, :]
    return (jnp.cos(angles), jnp.sin(angles))

def rotate(values, cosine_table, sine_table, head_dim):
    tok_rows = values.shape[0]
    head_count = values.shape[1] // head_dim
    shaped = values.reshape(tok_rows, head_count, head_dim)
    half_dim = head_dim // 2
    first_half = shaped[..., :half_dim]
    second = shaped[..., half_dim:]
    cos_b = cosine_table[:, None, :]
    sin_b = sine_table[:, None, :]
    turned = jnp.concatenate([first_half * cos_b - second * sin_b, second * cos_b + first_half * sin_b], axis=-1)
    return turned.reshape(tok_rows, head_count * head_dim)

def rms_scale(values, gain_vec):
    mean_square = lax.optimization_barrier(jnp.mean(values * values, axis=1))
    return values * lax.rsqrt(mean_square + norm_eps)[:, None] * gain_vec[None, :]

def reference(tokens, segment_ids, page_source, query_weight, key_weight, value_weight, out_weight, query_gain, key_gain, attention_gain, gate_weight, up_weight, down_weight, feedforward_gain):
    query_proj = jnp.dot(tokens, query_weight, preferred_element_type=jnp.float32)
    key_proj = jnp.dot(tokens, key_weight, preferred_element_type=jnp.float32)
    value_proj = jnp.dot(tokens, value_weight, preferred_element_type=jnp.float32)
    query_n = rms_scale(query_proj, query_gain)
    key_n = rms_scale(key_proj, key_gain)
    seg_range = jnp.arange(SEGS, dtype=jnp.int32)
    matches = segment_ids[:, None] == seg_range[None, :]
    counts = lax.optimization_barrier(jnp.sum(matches.astype(jnp.int32), axis=0)).astype(jnp.int32)
    seg_starts = (jnp.cumsum(counts) - counts).astype(jnp.int32)
    token_index = jnp.arange(TOKENS, dtype=jnp.int32)
    positions = (token_index - seg_starts[segment_ids]).astype(jnp.int32)
    cosine_table, sine_table = rope_tables(positions, HD)
    query_r = rotate(query_n, cosine_table, sine_table, HD).astype(jnp.bfloat16)
    key_r = rotate(key_n, cosine_table, sine_table, HD).astype(jnp.bfloat16)
    value_b = value_proj.astype(jnp.bfloat16)
    score_scale = HD ** (-0.5)
    query_heads = query_r.reshape(TOKENS, H, HD).transpose(1, 0, 2)
    key_heads = key_r.reshape(TOKENS, H, HD).transpose(1, 0, 2)
    value_heads = value_b.reshape(TOKENS, H, HD).transpose(1, 0, 2)
    block_count = TOKENS // TOK_DEV

    def one_head(operands):
        query_h, key_h, value_h = operands

        def one_block(block_index):
            offset = (block_index * TOK_DEV).astype(jnp.int32)
            query_b = lax.dynamic_slice_in_dim(query_h, offset, TOK_DEV, 0)
            seg_b = lax.dynamic_slice_in_dim(segment_ids, offset, TOK_DEV, 0)
            index_b = lax.dynamic_slice_in_dim(token_index, offset, TOK_DEV, 0)
            scores = jnp.dot(query_b, key_h.T, preferred_element_type=jnp.float32) * score_scale
            visible = (seg_b[:, None] == segment_ids[None, :]) & (index_b[:, None] >= token_index[None, :])
            top_score = lax.optimization_barrier(jnp.max(jnp.where(visible, scores, -1e+30), axis=1))
            weights = jnp.where(visible, jnp.exp(scores - top_score[:, None]), 0.0)
            denom = lax.optimization_barrier(jnp.sum(weights, axis=1))
            mixed = jnp.dot(weights.astype(jnp.bfloat16), value_h, preferred_element_type=jnp.float32)
            return (mixed / denom[:, None]).astype(jnp.bfloat16)
        blocks = lax.map(one_block, jnp.arange(block_count, dtype=jnp.int32))
        return blocks.reshape(TOKENS, HD)
    attended_heads = lax.map(one_head, (query_heads, key_heads, value_heads))
    attended = attended_heads.transpose(1, 0, 2).reshape(TOKENS, D)
    projected = jnp.dot(attended, out_weight, preferred_element_type=jnp.float32)
    residual = (tokens.astype(jnp.float32) + rms_scale(projected, attention_gain)).astype(jnp.bfloat16)
    gate_act = jnp.dot(residual, gate_weight, preferred_element_type=jnp.float32)
    up_act = jnp.dot(residual, up_weight, preferred_element_type=jnp.float32)
    hidden = (jax.nn.silu(gate_act) * up_act).astype(jnp.bfloat16)
    down_act = lax.dot_general(hidden, down_weight, (((1,), (1,)), ((), ())), preferred_element_type=jnp.float32)
    layer_out = (residual.astype(jnp.float32) + rms_scale(down_act, feedforward_gain)).astype(jnp.bfloat16)
    key_pages = key_r.reshape(PAGES, PAGE, D)[page_source]
    value_pages = value_b.reshape(PAGES, PAGE, D)[page_source]
    page_cache = jnp.stack([key_pages, value_pages], axis=1)
    return (layer_out, page_cache)
```

```python
import jax
import jax.numpy as jnp
from jax import lax
from jax.sharding import PartitionSpec as P

HD = 128
PAGE = 16
ZS = 8
XS = 4
YS = 4
RINGS = ZS * XS


rope_base = 500000.0
norm_eps = 1e-06


def rope_tables(positions, head_dim):
    half_dim = head_dim // 2
    inv_freq = rope_base ** (-(jnp.arange(half_dim, dtype=jnp.float32) * 2.0) / head_dim)
    angles = positions.astype(jnp.float32)[:, None] * inv_freq[None, :]
    return (jnp.cos(angles), jnp.sin(angles))


def rotate(values, cosine_table, sine_table, head_dim):
    tok_rows = values.shape[0]
    head_count = values.shape[1] // head_dim
    shaped = values.reshape(tok_rows, head_count, head_dim)
    half_dim = head_dim // 2
    first_half = shaped[..., :half_dim]
    second = shaped[..., half_dim:]
    cos_b = cosine_table[:, None, :]
    sin_b = sine_table[:, None, :]
    turned = jnp.concatenate(
        [first_half * cos_b - second * sin_b, second * cos_b + first_half * sin_b], axis=-1
    )
    return turned.reshape(tok_rows, head_count * head_dim)


def ring_shift(size, stride, step):
    pairs = []
    for src in range(RINGS):
        place = (src // stride) % size
        pairs.append((src, src + ((place + step) % size - place) * stride))
    return pairs


def ring_place(size, stride):
    return (lax.axis_index("req") // stride) % size


def ring_gather(piece, size, stride, put, state):
    place = ring_place(size, stride)
    state = put(state, piece, place, 0)
    ahead = behind = piece
    for step in range(1, size // 2):
        ahead = lax.ppermute(ahead, "req", ring_shift(size, stride, 1))
        behind = lax.ppermute(behind, "req", ring_shift(size, stride, -1))
        state = put(state, ahead, (place - step) % size, 0)
        state = put(state, behind, (place + step) % size, 0)
    half = piece.shape[0] // 2
    ahead = lax.ppermute(ahead[:half], "req", ring_shift(size, stride, 1))
    behind = lax.ppermute(behind[half:], "req", ring_shift(size, stride, -1))
    far = (place + size // 2) % size
    state = put(state, ahead, far, 0)
    return put(state, behind, far, half)


def gather_req(piece, z_first):
    rows, cols = piece.shape

    def put_line(state, part, place, row):
        return lax.dynamic_update_slice(state, part[None], (place, row, 0))

    def put_z(state, part, place, row):
        return lax.dynamic_update_slice(state, part[None], (place, row, 0, 0))

    def put_x(state, part, place, row):
        return lax.dynamic_update_slice(state, part[:, None], (row, place, 0, 0))

    whole = jnp.zeros((ZS, XS, rows, cols), piece.dtype)
    if z_first:
        line = ring_gather(piece, ZS, XS, put_line, jnp.zeros((ZS, rows, cols), piece.dtype))
        whole = ring_gather(line, XS, 1, put_x, whole)
    else:
        line = ring_gather(piece, XS, 1, put_line, jnp.zeros((XS, rows, cols), piece.dtype))
        whole = ring_gather(line, ZS, XS, put_z, whole)
    return whole.reshape(RINGS * rows, cols)


def gather_ids(segment_ids):
    rows = segment_ids.shape[0]
    own_z = ring_place(ZS, XS)
    own_x = ring_place(XS, 1)
    line = jnp.zeros((ZS, rows), jnp.int32)
    for step in range(ZS):
        part = lax.ppermute(segment_ids, "req", ring_shift(ZS, XS, step)) if step else segment_ids
        line = lax.dynamic_update_slice(line, part[None], ((own_z - step) % ZS, 0))
    whole = jnp.zeros((ZS, XS, rows), jnp.int32)
    for step in range(XS):
        part = lax.ppermute(line, "req", ring_shift(XS, 1, step)) if step else line
        whole = lax.dynamic_update_slice(whole, part[:, None], (0, (own_x - step) % XS, 0))
    return whole.reshape(-1)


def mlp_pairs(dy, dc):
    return [(m, ((m // 2 + dy) % YS) * 2 + (m % 2 ^ dc)) for m in range(2 * YS)]


def mlp_sum(values):
    total = values
    for dy in range(YS):
        for dc in range(2):
            if dy or dc:
                total = total + lax.ppermute(values, "mlp", mlp_pairs(dy, dc))
    return total


def mlp_gather(piece):
    rows, width = piece.shape
    own = lax.axis_index("mlp")
    own_y, own_c = own // 2, own % 2
    whole = jnp.zeros((rows, width * 2 * YS), piece.dtype)
    for dy in range(YS):
        part = lax.ppermute(piece, "mlp", mlp_pairs(dy, 0)) if dy else piece
        other = lax.ppermute(part, "mlp", mlp_pairs(0, 1))
        src_y = (own_y - dy) % YS
        whole = lax.dynamic_update_slice(whole, part, (0, (src_y * 2 + own_c) * width))
        whole = lax.dynamic_update_slice(whole, other, (0, (src_y * 2 + 1 - own_c) * width))
    return whole


def mlp_scatter_sum(values):
    rows = values.shape[0]
    width = values.shape[1] // (2 * YS)
    own = lax.axis_index("mlp")
    own_y, own_c = own // 2, own % 2
    total = None
    for dy in (2, 1, 3, 0):
        dst_y = (own_y + dy) % YS
        theirs = lax.dynamic_slice(values, (0, (dst_y * 2 + 1 - own_c) * width), (rows, width))
        mine = lax.dynamic_slice(values, (0, (dst_y * 2 + own_c) * width), (rows, width))
        got = lax.ppermute(theirs.astype(jnp.bfloat16), "mlp", mlp_pairs(0, 1))
        pair = mine + got.astype(jnp.float32)
        if dy:
            pair = lax.ppermute(pair.astype(jnp.bfloat16), "mlp", mlp_pairs(dy, 0))
            pair = pair.astype(jnp.float32)
        total = pair if total is None else total + pair
    return total


def post_norm(branch_term, gain_vec, model_width):
    own_part = mlp_scatter_sum(branch_term)
    mean_square = mlp_sum(jnp.sum(own_part * own_part, axis=1)) / model_width
    return own_part * lax.rsqrt(mean_square + norm_eps)[:, None] * gain_vec[None, :]


def per_device(
    tokens,
    segment_ids,
    page_source,
    query_weight,
    key_weight,
    value_weight,
    out_weight,
    query_gain,
    key_gain,
    attention_gain,
    gate_weight,
    up_weight,
    down_weight,
    feedforward_gain,
):
    tok_rows = tokens.shape[0]
    local_width = tokens.shape[1]
    model_width = query_weight.shape[0]
    head_dim = HD
    head_count = local_width // head_dim
    half_units = gate_weight.shape[1] // 2
    ffn_low = gather_req(
        jnp.concatenate([w[:, :half_units] for w in (gate_weight, up_weight, down_weight)], axis=1),
        True,
    )
    ffn_high = gather_req(
        jnp.concatenate([w[:, half_units:] for w in (gate_weight, up_weight, down_weight)], axis=1),
        False,
    )
    seg_part = gather_ids(segment_ids)
    full_rows = mlp_gather(tokens)
    query_proj = jnp.dot(full_rows, query_weight, preferred_element_type=jnp.float32)
    key_proj = jnp.dot(full_rows, key_weight, preferred_element_type=jnp.float32)
    value_proj = jnp.dot(full_rows, value_weight, preferred_element_type=jnp.float32)
    query_total, key_total = mlp_sum(
        jnp.stack([jnp.sum(query_proj * query_proj, axis=1), jnp.sum(key_proj * key_proj, axis=1)])
    )
    query_n = (
        query_proj * lax.rsqrt(query_total / model_width + norm_eps)[:, None] * query_gain[None, :]
    )
    key_n = key_proj * lax.rsqrt(key_total / model_width + norm_eps)[:, None] * key_gain[None, :]
    seg_total = lax.axis_size("req") // 2 + 1
    seg_range = jnp.arange(seg_total, dtype=jnp.int32)
    matches = segment_ids[:, None] == seg_range[None, :]
    seg_starts = jnp.sum((seg_part[:, None] < seg_range[None, :]).astype(jnp.int32), axis=0)
    row_base = lax.axis_index("req") * tok_rows
    global_index = row_base + jnp.arange(tok_rows, dtype=jnp.int32)
    own_start = jnp.sum(jnp.where(matches, seg_starts[None, :], 0), axis=1)
    positions = global_index - own_start
    cosine_table, sine_table = rope_tables(positions, head_dim)
    query_r = rotate(query_n, cosine_table, sine_table, head_dim).astype(jnp.bfloat16)
    key_r = rotate(key_n, cosine_table, sine_table, head_dim).astype(jnp.bfloat16)
    value_b = value_proj.astype(jnp.bfloat16)
    query_heads = query_r.reshape(tok_rows, head_count, head_dim)
    score_scale = head_dim ** (-0.5)
    pages_here = page_source.shape[0]
    page_offsets = jnp.arange(PAGE, dtype=jnp.int32)
    attn_init = (
        jnp.full((head_count, tok_rows), -1e30, jnp.float32),
        jnp.zeros((head_count, tok_rows), jnp.float32),
        jnp.zeros((tok_rows, head_count, head_dim), jnp.float32),
    )
    fetched = (gather_req(key_r, True), gather_req(value_b, False))
    key_part, value_part = fetched
    row_count = key_part.shape[0]
    block_rows = 512

    def one_block(block_index, state):
        run_max, run_sum, run_out = state
        offset = block_index * block_rows
        key_block = lax.dynamic_slice_in_dim(key_part, offset, block_rows, 0).reshape(
            block_rows, head_count, head_dim
        )
        value_block = lax.dynamic_slice_in_dim(value_part, offset, block_rows, 0).reshape(
            block_rows, head_count, head_dim
        )
        seg_block = lax.dynamic_slice_in_dim(seg_part, offset, block_rows, 0)
        key_index = offset + jnp.arange(block_rows, dtype=jnp.int32)
        visible = (
            (segment_ids[:, None] == seg_block[None, :])
            & (global_index[:, None] >= key_index[None, :])
            & (key_index[None, :] >= 0)
        )
        scores = (
            jnp.einsum("thd,rhd->htr", query_heads, key_block, preferred_element_type=jnp.float32)
            * score_scale
        )
        masked = jnp.where(visible[None], scores, -1e30)
        new_max = jnp.maximum(run_max, jnp.max(masked, axis=2))
        weights = jnp.where(visible[None], jnp.exp(scores - new_max[:, :, None]), 0.0)
        factor = jnp.exp(run_max - new_max)
        run_sum = run_sum * factor + jnp.sum(weights, axis=2)
        update = jnp.einsum(
            "htr,rhd->thd",
            weights.astype(jnp.bfloat16),
            value_block,
            preferred_element_type=jnp.float32,
        )
        run_out = run_out * factor.T[:, :, None] + update
        return (new_max, run_sum, run_out)

    first_block = own_start[0] // block_rows
    last_block = (row_base + tok_rows + block_rows - 1) // block_rows
    attn_state = lax.fori_loop(first_block, last_block, one_block, attn_init)
    page_rows = page_source[:, None] * PAGE + page_offsets[None, :]
    page_cache = jnp.stack([key_part[page_rows], value_part[page_rows]], axis=1)
    run_max, run_sum, run_out = attn_state
    attended = (run_out / run_sum.T[:, :, None]).reshape(tok_rows, local_width).astype(jnp.bfloat16)
    projected = jnp.dot(attended, out_weight, preferred_element_type=jnp.float32)
    residual = (
        tokens.astype(jnp.float32) + post_norm(projected, attention_gain, model_width)
    ).astype(jnp.bfloat16)
    normed = mlp_gather(residual)
    contract = (((1,), (1,)), ((), ()))
    down_act = None
    for part in (ffn_low, ffn_high):
        gate_act = jnp.dot(
            normed, part[:, :half_units], preferred_element_type=jnp.float32
        )
        up_act = jnp.dot(
            normed, part[:, half_units : 2 * half_units], preferred_element_type=jnp.float32
        )
        hidden = (jax.nn.silu(gate_act) * up_act).astype(jnp.bfloat16)
        down = lax.dot_general(
            hidden, part[:, 2 * half_units :], contract, preferred_element_type=jnp.float32
        )
        down_act = down if down_act is None else down_act + down
    layer_out = (
        residual.astype(jnp.float32) + post_norm(down_act, feedforward_gain, model_width)
    ).astype(jnp.bfloat16)
    return (layer_out, page_cache)


def solution(mesh):
    in_specs = (
        P("req", "mlp"),
        P("req"),
        P("req"),
        P(None, "mlp"),
        P(None, "mlp"),
        P(None, "mlp"),
        P("mlp", None),
        P("mlp"),
        P("mlp"),
        P("mlp"),
        P("req", "mlp"),
        P("req", "mlp"),
        P("req", "mlp"),
        P("mlp"),
    )
    out_specs = (P("req", "mlp"), P("req", None, None, "mlp"))
    return jax.shard_map(
        per_device, mesh=mesh, in_specs=in_specs, out_specs=out_specs, check_vma=False
    )
```

```python
import jax
import jax.numpy as jnp
from jax import lax
from jax.sharding import PartitionSpec as P

HD = 128
PAGE = 16
ZS = 8
XS = 4
YS = 4
RINGS = ZS * XS


rope_base = 500000.0
norm_eps = 1e-06


def rope_tables(positions, head_dim):
    half_dim = head_dim // 2
    inv_freq = rope_base ** (-(jnp.arange(half_dim, dtype=jnp.float32) * 2.0) / head_dim)
    angles = positions.astype(jnp.float32)[:, None] * inv_freq[None, :]
    return (jnp.cos(angles), jnp.sin(angles))


def rotate(values, cosine_table, sine_table, head_dim):
    tok_rows = values.shape[0]
    head_count = values.shape[1] // head_dim
    shaped = values.reshape(tok_rows, head_count, head_dim)
    half_dim = head_dim // 2
    first_half = shaped[..., :half_dim]
    second = shaped[..., half_dim:]
    cos_b = cosine_table[:, None, :]
    sin_b = sine_table[:, None, :]
    turned = jnp.concatenate(
        [first_half * cos_b - second * sin_b, second * cos_b + first_half * sin_b], axis=-1
    )
    return turned.reshape(tok_rows, head_count * head_dim)


def ring_shift(size, stride, step):
    pairs = []
    for src in range(RINGS):
        place = (src // stride) % size
        pairs.append((src, src + ((place + step) % size - place) * stride))
    return pairs


def ring_place(size, stride):
    return (lax.axis_index("req") // stride) % size


def ring_gather(piece, size, stride, put, state):
    place = ring_place(size, stride)
    state = put(state, piece, place, 0)
    ahead = behind = piece
    for step in range(1, size // 2):
        ahead = lax.ppermute(ahead, "req", ring_shift(size, stride, 1))
        behind = lax.ppermute(behind, "req", ring_shift(size, stride, -1))
        state = put(state, ahead, (place - step) % size, 0)
        state = put(state, behind, (place + step) % size, 0)
    half = piece.shape[0] // 2
    ahead = lax.ppermute(ahead[:half], "req", ring_shift(size, stride, 1))
    behind = lax.ppermute(behind[half:], "req", ring_shift(size, stride, -1))
    far = (place + size // 2) % size
    state = put(state, ahead, far, 0)
    return put(state, behind, far, half)


def gather_req(piece, z_first):
    rows, cols = piece.shape

    def put_line(state, part, place, row):
        return lax.dynamic_update_slice(state, part[None], (place, row, 0))

    def put_z(state, part, place, row):
        return lax.dynamic_update_slice(state, part[None], (place, row, 0, 0))

    def put_x(state, part, place, row):
        return lax.dynamic_update_slice(state, part[:, None], (row, place, 0, 0))

    whole = jnp.zeros((ZS, XS, rows, cols), piece.dtype)
    if z_first:
        line = ring_gather(piece, ZS, XS, put_line, jnp.zeros((ZS, rows, cols), piece.dtype))
        whole = ring_gather(line, XS, 1, put_x, whole)
    else:
        line = ring_gather(piece, XS, 1, put_line, jnp.zeros((XS, rows, cols), piece.dtype))
        whole = ring_gather(line, ZS, XS, put_z, whole)
    return whole.reshape(RINGS * rows, cols)


def mlp_pairs(dy, dc):
    return [(m, ((m // 2 + dy) % YS) * 2 + (m % 2 ^ dc)) for m in range(2 * YS)]


def exchange_sum(values, axis, size):
    bit = 1
    while bit < size:
        values = values + lax.ppermute(values, axis, [(m, m ^ bit) for m in range(size)])
        bit *= 2
    return values


def mlp_sum(values):
    return exchange_sum(values, "mlp", 2 * YS)


def mlp_gather(piece, axis):
    width = piece.shape[axis]
    own = lax.axis_index("mlp")
    own_y, own_c = own // 2, own % 2
    shape = list(piece.shape)
    shape[axis] = width * 2 * YS
    whole = jnp.zeros(shape, piece.dtype)
    for dy in range(YS):
        part = lax.ppermute(piece, "mlp", mlp_pairs(dy, 0)) if dy else piece
        other = lax.ppermute(part, "mlp", mlp_pairs(0, 1))
        src_y = (own_y - dy) % YS
        place = (src_y * 2 + own_c) * width
        whole = lax.dynamic_update_slice_in_dim(whole, part, place, axis)
        place = (src_y * 2 + 1 - own_c) * width
        whole = lax.dynamic_update_slice_in_dim(whole, other, place, axis)
    return whole


def mlp_scatter_sum(values):
    rows = values.shape[0]
    width = values.shape[1] // (2 * YS)
    own = lax.axis_index("mlp")
    own_y, own_c = own // 2, own % 2
    total = None
    for dy in (2, 1, 3, 0):
        dst_y = (own_y + dy) % YS
        theirs = lax.dynamic_slice(values, (0, (dst_y * 2 + 1 - own_c) * width), (rows, width))
        mine = lax.dynamic_slice(values, (0, (dst_y * 2 + own_c) * width), (rows, width))
        got = lax.ppermute(theirs.astype(jnp.bfloat16), "mlp", mlp_pairs(0, 1))
        pair = mine + got.astype(jnp.float32)
        if dy:
            pair = lax.ppermute(pair.astype(jnp.bfloat16), "mlp", mlp_pairs(dy, 0))
            pair = pair.astype(jnp.float32)
        total = pair if total is None else total + pair
    return total


def post_norm(branch_term, gain_vec, model_width):
    own_part = mlp_scatter_sum(branch_term)
    mean_square = mlp_sum(jnp.sum(own_part * own_part, axis=1)) / model_width
    return own_part * lax.rsqrt(mean_square + norm_eps)[:, None] * gain_vec[None, :]


def per_device(
    tokens,
    segment_ids,
    page_source,
    query_weight,
    key_weight,
    value_weight,
    out_weight,
    query_gain,
    key_gain,
    attention_gain,
    gate_weight,
    up_weight,
    down_weight,
    feedforward_gain,
):
    tok_rows = tokens.shape[0]
    local_width = tokens.shape[1]
    model_width = query_weight.shape[0]
    head_dim = HD
    head_count = local_width // head_dim
    seg_total = lax.axis_size("req") // 2 + 1
    seg_range = jnp.arange(seg_total, dtype=jnp.int32)
    matches = segment_ids[:, None] == seg_range[None, :]
    counts = jnp.sum(matches.astype(jnp.int32), axis=0)
    totals = exchange_sum(counts, "req", RINGS)
    units = gate_weight.shape[1]
    gate_up = lax.all_gather(
        jnp.concatenate([gate_weight, up_weight], axis=1), "req", axis=0, tiled=True
    )
    full_rows = mlp_gather(tokens, 1)
    query_proj = jnp.dot(full_rows, query_weight, preferred_element_type=jnp.float32)
    key_proj = jnp.dot(full_rows, key_weight, preferred_element_type=jnp.float32)
    value_proj = jnp.dot(full_rows, value_weight, preferred_element_type=jnp.float32)
    gain_row = jnp.arange(2 * YS, dtype=jnp.int32)[:, None] == lax.axis_index("mlp")
    shared = mlp_sum(
        jnp.concatenate(
            [
                jnp.sum(query_proj * query_proj, axis=1)[None],
                jnp.sum(key_proj * key_proj, axis=1)[None],
                jnp.where(gain_row, attention_gain[None, :], 0.0),
            ]
        )
    )
    query_total, key_total = shared[0], shared[1]
    full_gain = shared[2:].reshape(-1)
    query_n = (
        query_proj * lax.rsqrt(query_total / model_width + norm_eps)[:, None] * query_gain[None, :]
    )
    key_n = key_proj * lax.rsqrt(key_total / model_width + norm_eps)[:, None] * key_gain[None, :]
    seg_starts = jnp.cumsum(totals) - totals
    row_base = lax.axis_index("req") * tok_rows
    global_index = row_base + jnp.arange(tok_rows, dtype=jnp.int32)
    own_start = jnp.sum(jnp.where(matches, seg_starts[None, :], 0), axis=1)
    positions = global_index - own_start
    cosine_table, sine_table = rope_tables(positions, head_dim)
    query_r = rotate(query_n, cosine_table, sine_table, head_dim).astype(jnp.bfloat16)
    key_r = rotate(key_n, cosine_table, sine_table, head_dim).astype(jnp.bfloat16)
    value_b = value_proj.astype(jnp.bfloat16)
    out_rows, _ = lax.optimization_barrier((out_weight, query_total))
    out_full = mlp_gather(out_rows, 0)
    query_heads = query_r.reshape(tok_rows, head_count, head_dim)
    score_scale = head_dim ** (-0.5)
    pages_here = page_source.shape[0]
    page_offsets = jnp.arange(PAGE, dtype=jnp.int32)
    attn_init = (
        jnp.full((head_count, tok_rows), -1e30, jnp.float32),
        jnp.zeros((head_count, tok_rows), jnp.float32),
        jnp.zeros((tok_rows, head_count, head_dim), jnp.float32),
    )
    key_part, value_part = gather_req(key_r, True), gather_req(value_b, False)
    key_part, value_part, down_weight = lax.optimization_barrier(
        (key_part, value_part, down_weight)
    )
    half_units = units // 2
    down_low = gather_req(down_weight[:, :half_units], True)
    down_high = gather_req(down_weight[:, half_units:], False)
    row_count = key_part.shape[0]
    block_rows = 512

    def one_block(block_index, state):
        run_max, run_sum, run_out = state
        offset = block_index * block_rows
        key_block = lax.dynamic_slice_in_dim(key_part, offset, block_rows, 0).reshape(
            block_rows, head_count, head_dim
        )
        value_block = lax.dynamic_slice_in_dim(value_part, offset, block_rows, 0).reshape(
            block_rows, head_count, head_dim
        )
        key_index = offset + jnp.arange(block_rows, dtype=jnp.int32)
        visible = (
            (own_start[:, None] <= key_index[None, :])
            & (global_index[:, None] >= key_index[None, :])
        )
        scores = (
            jnp.einsum("thd,rhd->htr", query_heads, key_block, preferred_element_type=jnp.float32)
            * score_scale
        )
        masked = jnp.where(visible[None], scores, -1e30)
        new_max = jnp.maximum(run_max, jnp.max(masked, axis=2))
        weights = jnp.where(visible[None], jnp.exp(scores - new_max[:, :, None]), 0.0)
        factor = jnp.exp(run_max - new_max)
        run_sum = run_sum * factor + jnp.sum(weights, axis=2)
        update = jnp.einsum(
            "htr,rhd->thd",
            weights.astype(jnp.bfloat16),
            value_block,
            preferred_element_type=jnp.float32,
        )
        run_out = run_out * factor.T[:, :, None] + update
        return (new_max, run_sum, run_out)

    first_block = own_start[0] // block_rows
    last_block = (row_base + tok_rows + block_rows - 1) // block_rows
    attn_state = lax.fori_loop(first_block, last_block, one_block, attn_init)
    page_rows = page_source[:, None] * PAGE + page_offsets[None, :]
    page_cache = jnp.stack([key_part[page_rows], value_part[page_rows]], axis=1)
    run_max, run_sum, run_out = attn_state
    attended = (run_out / run_sum.T[:, :, None]).reshape(tok_rows, local_width).astype(jnp.bfloat16)
    projected = jnp.dot(
        mlp_gather(attended, 1), out_full, preferred_element_type=jnp.float32
    )
    mean_square = jnp.sum(projected * projected, axis=1) / model_width
    normed = (
        full_rows.astype(jnp.float32)
        + projected * lax.rsqrt(mean_square + norm_eps)[:, None] * full_gain[None, :]
    ).astype(jnp.bfloat16)
    residual = lax.dynamic_slice_in_dim(
        normed, lax.axis_index("mlp") * local_width, local_width, 1
    )
    contract = (((1,), (1,)), ((), ()))
    gate_act = jnp.dot(normed, gate_up[:, :units], preferred_element_type=jnp.float32)
    up_act = jnp.dot(normed, gate_up[:, units:], preferred_element_type=jnp.float32)
    hidden = (jax.nn.silu(gate_act) * up_act).astype(jnp.bfloat16)
    down_act = lax.dot_general(
        hidden[:, :half_units], down_low, contract, preferred_element_type=jnp.float32
    ) + lax.dot_general(
        hidden[:, half_units:], down_high, contract, preferred_element_type=jnp.float32
    )
    layer_out = (
        residual.astype(jnp.float32) + post_norm(down_act, feedforward_gain, model_width)
    ).astype(jnp.bfloat16)
    return (layer_out, page_cache)


def solution(mesh):
    in_specs = (
        P("req", "mlp"),
        P("req"),
        P("req"),
        P(None, "mlp"),
        P(None, "mlp"),
        P(None, "mlp"),
        P("mlp", None),
        P("mlp"),
        P("mlp"),
        P("mlp"),
        P("req", "mlp"),
        P("req", "mlp"),
        P("req", "mlp"),
        P("mlp"),
    )
    out_specs = (P("req", "mlp"), P("req", None, None, "mlp"))
    return jax.shard_map(
        per_device, mesh=mesh, in_specs=in_specs, out_specs=out_specs, check_vma=False
    )
```

```python
import jax
import jax.numpy as jnp
from jax import lax
from jax.sharding import PartitionSpec as P

HD = 128
PAGE = 16
ZS = 8
XS = 4
YS = 4
RINGS = ZS * XS


rope_base = 500000.0
norm_eps = 1e-06


def rope_tables(positions, head_dim):
    half_dim = head_dim // 2
    inv_freq = rope_base ** (-(jnp.arange(half_dim, dtype=jnp.float32) * 2.0) / head_dim)
    angles = positions.astype(jnp.float32)[:, None] * inv_freq[None, :]
    return (jnp.cos(angles), jnp.sin(angles))


def rotate(values, cosine_table, sine_table, head_dim):
    tok_rows = values.shape[0]
    head_count = values.shape[1] // head_dim
    shaped = values.reshape(tok_rows, head_count, head_dim)
    half_dim = head_dim // 2
    first_half = shaped[..., :half_dim]
    second = shaped[..., half_dim:]
    cos_b = cosine_table[:, None, :]
    sin_b = sine_table[:, None, :]
    turned = jnp.concatenate(
        [first_half * cos_b - second * sin_b, second * cos_b + first_half * sin_b], axis=-1
    )
    return turned.reshape(tok_rows, head_count * head_dim)


def ring_shift(size, stride, step):
    pairs = []
    for src in range(RINGS):
        place = (src // stride) % size
        pairs.append((src, src + ((place + step) % size - place) * stride))
    return pairs


def ring_place(size, stride):
    return (lax.axis_index("req") // stride) % size


def ring_gather(piece, size, stride, put, state):
    place = ring_place(size, stride)
    state = put(state, piece, place, 0)
    ahead = behind = piece
    for step in range(1, size // 2):
        ahead = lax.ppermute(ahead, "req", ring_shift(size, stride, 1))
        behind = lax.ppermute(behind, "req", ring_shift(size, stride, -1))
        state = put(state, ahead, (place - step) % size, 0)
        state = put(state, behind, (place + step) % size, 0)
    half = piece.shape[0] // 2
    ahead = lax.ppermute(ahead[:half], "req", ring_shift(size, stride, 1))
    behind = lax.ppermute(behind[half:], "req", ring_shift(size, stride, -1))
    far = (place + size // 2) % size
    state = put(state, ahead, far, 0)
    return put(state, behind, far, half)


def gather_req(piece, z_first):
    rows, cols = piece.shape

    def put_line(state, part, place, row):
        return lax.dynamic_update_slice(state, part[None], (place, row, 0))

    def put_z(state, part, place, row):
        return lax.dynamic_update_slice(state, part[None], (place, row, 0, 0))

    def put_x(state, part, place, row):
        return lax.dynamic_update_slice(state, part[:, None], (row, place, 0, 0))

    whole = jnp.zeros((ZS, XS, rows, cols), piece.dtype)
    if z_first:
        line = ring_gather(piece, ZS, XS, put_line, jnp.zeros((ZS, rows, cols), piece.dtype))
        whole = ring_gather(line, XS, 1, put_x, whole)
    else:
        line = ring_gather(piece, XS, 1, put_line, jnp.zeros((XS, rows, cols), piece.dtype))
        whole = ring_gather(line, ZS, XS, put_z, whole)
    return whole.reshape(RINGS * rows, cols)


def mlp_pairs(dy, dc):
    return [(m, ((m // 2 + dy) % YS) * 2 + (m % 2 ^ dc)) for m in range(2 * YS)]


def exchange_sum(values, axis, size):
    bit = 1
    while bit < size:
        values = values + lax.ppermute(values, axis, [(m, m ^ bit) for m in range(size)])
        bit *= 2
    return values


def mlp_sum(values):
    return exchange_sum(values, "mlp", 2 * YS)


def mlp_gather(piece, axis, after=None):
    width = piece.shape[axis]
    own = lax.axis_index("mlp")
    own_y, own_c = own // 2, own % 2
    shape = list(piece.shape)
    shape[axis] = width * 2 * YS
    whole = jnp.zeros(shape, piece.dtype)
    parts = [lax.ppermute(piece, "mlp", mlp_pairs(dy, 0)) if dy else piece for dy in range(YS)]
    if after is not None:
        parts, _ = lax.optimization_barrier((parts, after))
    for dy, part in enumerate(parts):
        other = lax.ppermute(part, "mlp", mlp_pairs(0, 1))
        src_y = (own_y - dy) % YS
        place = (src_y * 2 + own_c) * width
        whole = lax.dynamic_update_slice_in_dim(whole, part, place, axis)
        place = (src_y * 2 + 1 - own_c) * width
        whole = lax.dynamic_update_slice_in_dim(whole, other, place, axis)
    return whole


def mlp_scatter_sum(values):
    rows = values.shape[0]
    width = values.shape[1] // (2 * YS)
    own = lax.axis_index("mlp")
    own_y, own_c = own // 2, own % 2
    total = None
    for dy in (2, 1, 3, 0):
        dst_y = (own_y + dy) % YS
        theirs = lax.dynamic_slice(values, (0, (dst_y * 2 + 1 - own_c) * width), (rows, width))
        mine = lax.dynamic_slice(values, (0, (dst_y * 2 + own_c) * width), (rows, width))
        got = lax.ppermute(theirs.astype(jnp.bfloat16), "mlp", mlp_pairs(0, 1))
        pair = mine + got.astype(jnp.float32)
        if dy:
            pair = lax.ppermute(pair.astype(jnp.bfloat16), "mlp", mlp_pairs(dy, 0))
            pair = pair.astype(jnp.float32)
        total = pair if total is None else total + pair
    return total


def post_norm(branch_term, gain_vec, model_width):
    own_part = mlp_scatter_sum(branch_term)
    mean_square = mlp_sum(jnp.sum(own_part * own_part, axis=1)) / model_width
    return own_part * lax.rsqrt(mean_square + norm_eps)[:, None] * gain_vec[None, :]


def per_device(
    tokens,
    segment_ids,
    page_source,
    query_weight,
    key_weight,
    value_weight,
    out_weight,
    query_gain,
    key_gain,
    attention_gain,
    gate_weight,
    up_weight,
    down_weight,
    feedforward_gain,
):
    tok_rows = tokens.shape[0]
    local_width = tokens.shape[1]
    model_width = query_weight.shape[0]
    head_dim = HD
    head_count = local_width // head_dim
    seg_total = lax.axis_size("req") // 2 + 1
    seg_range = jnp.arange(seg_total, dtype=jnp.int32)
    matches = segment_ids[:, None] == seg_range[None, :]
    counts = jnp.sum(matches.astype(jnp.int32), axis=0)
    totals = exchange_sum(counts, "req", RINGS)
    units = gate_weight.shape[1]
    gate_up = lax.all_gather(
        jnp.concatenate([gate_weight, up_weight], axis=1), "req", axis=0, tiled=True
    )
    down_full = lax.all_gather(down_weight, "req", axis=0, tiled=True)
    full_rows = mlp_gather(tokens, 1)
    query_proj = jnp.dot(full_rows, query_weight, preferred_element_type=jnp.float32)
    key_proj = jnp.dot(full_rows, key_weight, preferred_element_type=jnp.float32)
    value_proj = jnp.dot(full_rows, value_weight, preferred_element_type=jnp.float32)
    gain_row = jnp.arange(2 * YS, dtype=jnp.int32)[:, None] == lax.axis_index("mlp")
    shared = mlp_sum(
        jnp.concatenate(
            [
                jnp.sum(query_proj * query_proj, axis=1)[None],
                jnp.sum(key_proj * key_proj, axis=1)[None],
                jnp.where(gain_row, attention_gain[None, :], 0.0),
            ]
        )
    )
    query_total, key_total = shared[0], shared[1]
    full_gain = shared[2:].reshape(-1)
    query_n = (
        query_proj * lax.rsqrt(query_total / model_width + norm_eps)[:, None] * query_gain[None, :]
    )
    key_n = key_proj * lax.rsqrt(key_total / model_width + norm_eps)[:, None] * key_gain[None, :]
    seg_starts = jnp.cumsum(totals) - totals
    row_base = lax.axis_index("req") * tok_rows
    global_index = row_base + jnp.arange(tok_rows, dtype=jnp.int32)
    own_start = jnp.sum(jnp.where(matches, seg_starts[None, :], 0), axis=1)
    positions = global_index - own_start
    cosine_table, sine_table = rope_tables(positions, head_dim)
    query_r = rotate(query_n, cosine_table, sine_table, head_dim).astype(jnp.bfloat16)
    key_r = rotate(key_n, cosine_table, sine_table, head_dim).astype(jnp.bfloat16)
    value_b = value_proj.astype(jnp.bfloat16)
    query_heads = query_r.reshape(tok_rows, head_count, head_dim)
    score_scale = head_dim ** (-0.5)
    pages_here = page_source.shape[0]
    page_offsets = jnp.arange(PAGE, dtype=jnp.int32)
    attn_init = (
        jnp.full((head_count, tok_rows), -1e30, jnp.float32),
        jnp.zeros((head_count, tok_rows), jnp.float32),
        jnp.zeros((tok_rows, head_count, head_dim), jnp.float32),
    )
    key_part, value_part = gather_req(key_r, True), gather_req(value_b, False)
    out_full = mlp_gather(out_weight, 0, key_part)
    row_count = key_part.shape[0]
    block_rows = 512

    def one_block(block_index, state):
        run_max, run_sum, run_out = state
        offset = block_index * block_rows
        key_block = lax.dynamic_slice_in_dim(key_part, offset, block_rows, 0).reshape(
            block_rows, head_count, head_dim
        )
        value_block = lax.dynamic_slice_in_dim(value_part, offset, block_rows, 0).reshape(
            block_rows, head_count, head_dim
        )
        key_index = offset + jnp.arange(block_rows, dtype=jnp.int32)
        visible = (
            (own_start[:, None] <= key_index[None, :])
            & (global_index[:, None] >= key_index[None, :])
        )
        scores = (
            jnp.einsum("thd,rhd->htr", query_heads, key_block, preferred_element_type=jnp.float32)
            * score_scale
        )
        masked = jnp.where(visible[None], scores, -1e30)
        new_max = jnp.maximum(run_max, jnp.max(masked, axis=2))
        weights = jnp.where(visible[None], jnp.exp(scores - new_max[:, :, None]), 0.0)
        factor = jnp.exp(run_max - new_max)
        run_sum = run_sum * factor + jnp.sum(weights, axis=2)
        update = jnp.einsum(
            "htr,rhd->thd",
            weights.astype(jnp.bfloat16),
            value_block,
            preferred_element_type=jnp.float32,
        )
        run_out = run_out * factor.T[:, :, None] + update
        return (new_max, run_sum, run_out)

    first_block = own_start[0] // block_rows
    last_block = (row_base + tok_rows + block_rows - 1) // block_rows
    attn_state = lax.fori_loop(first_block, last_block, one_block, attn_init)
    page_rows = page_source[:, None] * PAGE + page_offsets[None, :]
    page_cache = jnp.stack([key_part[page_rows], value_part[page_rows]], axis=1)
    run_max, run_sum, run_out = attn_state
    attended = (run_out / run_sum.T[:, :, None]).reshape(tok_rows, local_width).astype(jnp.bfloat16)
    projected = jnp.dot(
        mlp_gather(attended, 1), out_full, preferred_element_type=jnp.float32
    )
    mean_square = jnp.sum(projected * projected, axis=1) / model_width
    normed = (
        full_rows.astype(jnp.float32)
        + projected * lax.rsqrt(mean_square + norm_eps)[:, None] * full_gain[None, :]
    ).astype(jnp.bfloat16)
    residual = lax.dynamic_slice_in_dim(
        normed, lax.axis_index("mlp") * local_width, local_width, 1
    )
    contract = (((1,), (1,)), ((), ()))
    gate_act = jnp.dot(normed, gate_up[:, :units], preferred_element_type=jnp.float32)
    up_act = jnp.dot(normed, gate_up[:, units:], preferred_element_type=jnp.float32)
    hidden = (jax.nn.silu(gate_act) * up_act).astype(jnp.bfloat16)
    down_act = lax.dot_general(
        hidden, down_full, contract, preferred_element_type=jnp.float32
    )
    layer_out = (
        residual.astype(jnp.float32) + post_norm(down_act, feedforward_gain, model_width)
    ).astype(jnp.bfloat16)
    return (layer_out, page_cache)


def solution(mesh):
    in_specs = (
        P("req", "mlp"),
        P("req"),
        P("req"),
        P(None, "mlp"),
        P(None, "mlp"),
        P(None, "mlp"),
        P("mlp", None),
        P("mlp"),
        P("mlp"),
        P("mlp"),
        P("req", "mlp"),
        P("req", "mlp"),
        P("req", "mlp"),
        P("mlp"),
    )
    out_specs = (P("req", "mlp"), P("req", None, None, "mlp"))
    return jax.shard_map(
        per_device, mesh=mesh, in_specs=in_specs, out_specs=out_specs, check_vma=False
    )
```
